32 devices in a mesh: col: 4 (over y, x), row: 8 (over z, core).
Axes of the slice: x: 2, y: 2, z: 4, core: 2. Of those that a mesh axis runs over, the one named last changes fastest.
Arguments:
- weights: float32 [16384, 16384], P('row', 'col'), may hold values from -6 to 6
- factor_rows: bfloat16 [1024, 16384], P('row', 'col'), may hold values from -0.25 to 0.25
- diag_inverse: bfloat16 [8, 128, 128], replicated, as said below
- prune_tiles: int32 [128, 8], P('row'), may hold values 0 or 1
- pivot_order: int32 [8], replicated, may hold values from 0 to 127, as said below
Outputs:
- pruned_weights: float32 [16384, 16384], P('row', 'col')
The draws below stay inside these ranges and needn't reach their ends.
Inputs may be any that keep to these rules, and one draw needn't show every extreme that they name: `pivot_order`: the 8 block numbers are distinct; block 0 and the last block are among them. `diag_inverse`: each block is upper triangular with positive diagonal.
All inputs are finite; a program needn't handle non-finite values. No bound on the sum of `prune_tiles` on one device may be relied on, other than what follows from the above.
Results may differ from the reference program's by a relative error of at most 0.0003.
Values may be sent and summed in bfloat16 or wider, within the bound.
No kernel may reach another device: no remote copies, remote signals or barrier semaphores. Data moves between devices by JAX's collectives and lax.ppermute only.
A program may use at most 192 MiB of HBM per device.

```python
import jax
import jax.numpy as jnp
from jax import lax

ROWS = 16384
COLS = 16384
BLOCK = 128
PIVOTS = 8


def draw_pivot_order(key, part):
    nblocks = COLS // BLOCK
    first, second = jax.random.split(jax.random.fold_in(key, 29))
    middle = jax.random.permutation(first, nblocks - 2)[:PIVOTS - 2].astype(jnp.int32) + 1
    chosen = jnp.concatenate([jnp.zeros((1,), jnp.int32), jnp.full((1,), nblocks - 1, jnp.int32), middle])
    return jax.random.permutation(second, chosen).astype(jnp.int32)


def draw_diag_inverse(key, part):
    first, second = jax.random.split(jax.random.fold_in(key, 17))
    diagonal = jnp.exp(jax.random.uniform(first, (PIVOTS, BLOCK), jnp.float32, jnp.log(0.5), jnp.log(2.0)))
    offdiag = 0.5 * jax.random.normal(second, (PIVOTS, BLOCK, BLOCK), jnp.float32) / jnp.sqrt(jnp.float32(BLOCK))
    upper = jnp.triu(offdiag, 1) + diagonal[:, :, None] * jnp.eye(BLOCK, dtype=jnp.float32)[None]
    return upper.astype(jnp.bfloat16)


def place_ends(result, key, least, high):
    place = [jax.random.randint(jax.random.fold_in(key, axis), (), 0, length) for axis, length in enumerate(result.shape)]
    longest = result.shape.index(max(result.shape))
    beside = place[:longest] + [(place[longest] + 1) % result.shape[longest]] + place[longest + 1:]
    return result.at[tuple(place)].set(least).at[tuple(beside)].set(high)


def steps_of(key, dims, shards, least, top_value):
    gain = 1.0
    for axis_at, blocks in shards:
        heights = jax.random.uniform(jax.random.fold_in(jax.random.fold_in(key, 6), axis_at), (blocks,), jnp.float32, least / len(shards), top_value / len(shards))
        gain = gain * jnp.repeat(jnp.exp(heights), dims[axis_at] // blocks).reshape((-1,) + (1,) * (len(dims) - 1 - axis_at))
    return gain


def bell_draw(own_key, shape, width, reach, shards=(), kind=jnp.bfloat16):
    drawn = jax.random.normal(own_key, shape, jnp.float32) * width
    if len(shards) > 0:
        drawn = steps_of(own_key, shape, shards, -0.22, 0.18) * drawn
    return jnp.clip(drawn, min=-reach, max=reach).astype(kind)


def setup_inputs(seed: int = 0) -> dict:
    key_list = jax.random.split(jax.random.key(seed), 6)
    return {
        "weights": bell_draw(key_list[0], (ROWS, COLS), 1.0, 6.0, ((0, 8), (1, 4)), jnp.float32),
        "factor_rows": bell_draw(key_list[1], (PIVOTS * BLOCK, COLS), (4 * BLOCK) ** -0.5, 0.25, ((0, 8), (1, 4))),
        "diag_inverse": draw_diag_inverse(jax.random.fold_in(key_list[5], 71), 0),
        "prune_tiles": place_ends((jax.random.randint(key_list[3], (ROWS // BLOCK, PIVOTS), 0, 2) < 1).astype(jnp.int32), jax.random.fold_in(key_list[3], 1), 0, 1),
        "pivot_order": draw_pivot_order(jax.random.fold_in(key_list[5], 71), 0),
    }


def reference(weights, factor_rows, diag_inverse, prune_tiles, pivot_order):
    nblocks = COLS // BLOCK
    current = weights
    finished = jnp.zeros((nblocks,), jnp.float32)
    block_ids = jnp.arange(nblocks, dtype=jnp.int32)
    pruned_all = jnp.repeat(prune_tiles.astype(jnp.float32), BLOCK, axis=0)
    for step in range(PIVOTS):
        block_id = pivot_order[step]
        start = (block_id * BLOCK).astype(jnp.int32)
        panel_now = lax.dynamic_slice_in_dim(current, start, BLOCK, 1)
        pruned = pruned_all[:, step:step + 1]
        errors = jnp.dot(panel_now, diag_inverse[step].astype(jnp.float32), precision=lax.Precision.HIGHEST) * pruned
        finished = jnp.maximum(finished, (block_ids == block_id).astype(jnp.float32))
        keep_cols = jnp.repeat(1.0 - finished, BLOCK)
        update = jnp.dot(errors, factor_rows[step * BLOCK:(step + 1) * BLOCK].astype(jnp.float32), precision=lax.Precision.HIGHEST)
        current = current - update * keep_cols[None, :]
        current = lax.dynamic_update_slice_in_dim(current, panel_now * (1.0 - pruned), start, 1)
    return current
```

```python
import functools

import jax
import jax.numpy as jnp
from jax import lax
from jax.experimental import pallas as pl
from jax.experimental.pallas import tpu as pltpu
from jax.sharding import PartitionSpec as P


F32 = jnp.float32
BF16 = jnp.bfloat16
TOP = 32767.0
TAIL = 16
TILE = 256


def eye_of(n):
    return lax.broadcasted_iota(jnp.int32, (n, n), 0) == lax.broadcasted_iota(jnp.int32, (n, n), 1)


def pack_kernel(block, half, idx_ref, w_ref, a_ref, b_ref):
    for part, out in enumerate((a_ref, b_ref)):
        x = w_ref[part * half : (part + 1) * half, :]
        top = jnp.maximum(jnp.max(jnp.abs(x), axis=1, keepdims=True), 1e-30)
        level = jnp.ceil(jnp.log2(top))
        coded = jnp.clip(jnp.round(x * (TOP * jnp.exp2(-level))), -TOP, TOP)
        out[0, :half, :] = coded.astype(jnp.int32).astype(jnp.int16)
        tail = jnp.zeros((TAIL, block), F32)
        row = lax.broadcasted_iota(jnp.int32, (TAIL, block), 0)
        for t in range(half // block):
            spread = jnp.where(eye_of(block), level[t * block : (t + 1) * block], 0.0)
            line = jnp.sum(spread, axis=0, keepdims=True)
            tail = jnp.where(row == t, line, tail)
        out[0, half:, :] = tail.astype(jnp.int32).astype(jnp.int16)


def pack(weights, index, count, block, part):
    rows = weights.shape[0] // 2
    half = rows // 2
    shape = jax.ShapeDtypeStruct((count, half + TAIL, block), jnp.int16)
    return pl.pallas_call(
        functools.partial(pack_kernel, block, half),
        grid_spec=pltpu.PrefetchScalarGridSpec(
            num_scalar_prefetch=1,
            grid=(count,),
            in_specs=[pl.BlockSpec((rows, block), lambda m, idx: (part, idx[m]))],
            out_specs=[pl.BlockSpec((1, half + TAIL, block), lambda m, idx: (m, 0, 0))] * 2,
        ),
        out_shape=[shape, shape],
        name="pack",
    )(index, weights)


def gather_rows(chip, core, chips, shard, pieces, span, target, sems):
    own, sown, far, sfar = pieces
    todo = [(own.at[:, span], chip * 2 + core), (sown.at[:, span], chip * 2 + 1 - core)]
    for q in range(chips - 1):
        there = lax.rem(chip - q - 1 + chips, chips)
        todo.append((far.at[pl.ds(q * shard, shard), :], there * 2 + core))
        todo.append((sfar.at[pl.ds(q * shard, shard), :], there * 2 + 1 - core))
    return [
        pltpu.make_async_copy(
            src, target.at[pl.ds(pl.multiple_of(at * shard, shard), shard), :], sems.at[n]
        )
        for n, (src, at) in enumerate(todo)
    ]


def chain_kernel(geo, *refs):
    groups, n_rel, count, pivots, block, tile, half, shard, base = geo
    rel_ref, rank_ref, tiles_ref, where_ref = refs[:4]
    n_src = groups * 2 * n_rel
    sources = refs[4 : 4 + n_src]
    f_pieces = refs[4 + n_src : 8 + n_src]
    d_ref, hi_ref, lo_ref, coded, tails, cur, f_all, sems, f_sems = refs[8 + n_src :]
    step = pl.program_id(0)
    per_half = half // tile
    sub = tile // block
    depth = pivots * block
    chips = depth // shard // 2
    first = pl.multiple_of(lax.rem(step, per_half) * tile, tile)

    def f_copies():
        return gather_rows(
            where_ref[0], where_ref[1], chips, shard, f_pieces, pl.ds(0, depth), f_all, f_sems
        )

    @pl.when(step == 0)
    def _():
        for copy in f_copies():
            copy.start()

    def copies(k, ref):
        rank = lax.rem(rank_ref[k], count)
        return (
            pltpu.make_async_copy(ref.at[rank, pl.ds(first, tile), :], coded.at[k], sems.at[0, k]),
            pltpu.make_async_copy(ref.at[rank, pl.ds(half, TAIL), :], tails.at[k], sems.at[1, k]),
        )

    @pl.loop(0, pivots)
    def _(k):
        for group in range(groups):
            for part in range(2):
                for rel in range(n_rel):
                    ref = sources[(group * 2 + part) * n_rel + rel]
                    here = (step // per_half == part) & (rel_ref[k] == rel)

                    @pl.when(here & (rank_ref[k] // count == group))
                    def _(ref=ref):
                        for copy in copies(k, ref):
                            copy.start()

    eye = eye_of(block)
    row = lax.broadcasted_iota(jnp.int32, (TAIL, block), 0)
    for k in range(pivots):
        for copy in copies(k, sources[0]):
            copy.wait()
        tail = tails[k].astype(jnp.int32).astype(F32)
        for t in range(sub):
            here = lax.rem(step, per_half) * sub + t
            line = jnp.sum(jnp.where(row == here, tail, 0.0), axis=0, keepdims=True)
            level = jnp.sum(jnp.where(eye, line, 0.0), axis=1, keepdims=True)
            span = slice(t * block, (t + 1) * block)
            value = coded[k, span, :].astype(jnp.int32).astype(F32)
            cur[span, k * block : (k + 1) * block] = value * (jnp.exp2(level) * (1.0 / TOP))

    @pl.when(step == 0)
    def _():
        for copy in f_copies():
            copy.wait()

    for k in range(pivots):
        cols = slice(k * block, (k + 1) * block)
        now = cur[:, cols]
        now_hi = now.astype(BF16)
        now_lo = (now - now_hi.astype(F32)).astype(BF16)
        diag = d_ref[k]
        err = jnp.dot(
            jnp.concatenate([now_hi, now_lo], axis=1),
            jnp.concatenate([diag, diag], axis=0),
            preferred_element_type=F32,
        )
        parts = []
        for t in range(sub):
            flag = tiles_ref[base + step * sub + t, k].astype(F32)
            parts.append(err[t * block : (t + 1) * block] * flag)
        err = jnp.concatenate(parts, axis=0)
        hi = err.astype(BF16)
        lo = (err - hi.astype(F32)).astype(BF16)
        hi_ref[:, cols] = hi
        lo_ref[:, cols] = lo
        if k + 1 < pivots:
            f = f_all[cols, (k + 1) * block :]
            both = jnp.concatenate([hi, lo], axis=1)
            cur[:, (k + 1) * block :] -= jnp.dot(
                both, jnp.concatenate([f, f], axis=0), preferred_element_type=F32
            )


def chain(count, rel, rank, tiles, where, sources, f_pieces, diag, rows, shard, part):
    pivots, block, _ = diag.shape
    half = rows // 2
    tile = min(512, half)
    groups = len(sources)
    n_rel = len(sources[0]) // 2
    flat = [x for group in sources for x in group]
    depth = pivots * block
    shape = jax.ShapeDtypeStruct((rows, depth), BF16)
    anywhere = pl.BlockSpec(memory_space=pl.ANY)
    geo = (groups, n_rel, count, pivots, block, tile, half, shard, part * rows // block)
    return pl.pallas_call(
        functools.partial(chain_kernel, geo),
        grid_spec=pltpu.PrefetchScalarGridSpec(
            num_scalar_prefetch=4,
            grid=(rows // tile,),
            in_specs=[anywhere] * (len(flat) + 4)
            + [pl.BlockSpec(diag.shape, lambda i, *_: (0, 0, 0))],
            out_specs=[pl.BlockSpec((tile, depth), lambda i, *_: (i, 0))] * 2,
            scratch_shapes=[
                pltpu.VMEM((pivots, tile, block), jnp.int16),
                pltpu.VMEM((pivots, TAIL, block), jnp.int16),
                pltpu.VMEM((tile, depth), F32),
                pltpu.VMEM((depth, depth), BF16),
                pltpu.SemaphoreType.DMA((2, pivots)),
                pltpu.SemaphoreType.DMA((depth // shard,)),
            ],
        ),
        out_shape=[shape, shape],
        cost_estimate=pl.CostEstimate(
            flops=4 * rows * depth * depth, bytes_accessed=8 * rows * depth, transcendentals=0
        ),
        name="chain",
    )(rel, rank, tiles, where, *flat, *f_pieces, diag)


def pick_kernel(local_ref, mine_ref, f_ref, o_ref):
    k = pl.program_id(0)
    o_ref[...] = (f_ref[...].astype(F32) * mine_ref[k].astype(F32)).astype(BF16)


def pick(factor_rows, local, mine, block):
    shard = factor_rows.shape[0]
    pivots = local.shape[0]
    return pl.pallas_call(
        pick_kernel,
        grid_spec=pltpu.PrefetchScalarGridSpec(
            num_scalar_prefetch=2,
            grid=(pivots,),
            in_specs=[pl.BlockSpec((shard, block), lambda k, local, mine: (0, local[k]))],
            out_specs=pl.BlockSpec((shard, block), lambda k, *_: (0, k)),
        ),
        out_shape=jax.ShapeDtypeStruct((shard, pivots * block), BF16),
        name="pick",
    )(local, mine, factor_rows)


def main_kernel(geo, where_ref, kind_ref, tiles_ref, hi_ref, lo_ref, w_ref, *refs):
    block, pivots, shard, chips, width, tile, offset, base = geo
    own, sown, far, sfar = refs[:4]
    o_ref, f, sems = refs[-3:]
    step = pl.program_id(0)
    chip = where_ref[0]
    core = where_ref[1]

    def pieces():
        return gather_rows(chip, core, chips, shard, (own, sown, far, sfar), pl.ds(offset, width), f, sems)

    @pl.when(step == 0)
    def _():
        for copy in pieces():
            copy.start()
        for copy in pieces():
            copy.wait()
        row = lax.broadcasted_iota(jnp.int32, (pivots * block, block), 0)
        for b in range(width // block):
            kind = kind_ref[offset // block + b]

            @pl.when(kind < pivots)
            def _(b=b, kind=kind):
                cols = slice(b * block, (b + 1) * block)
                f[:, cols] = jnp.where(row < kind * block, f[:, cols].astype(F32), 0.0).astype(BF16)

    acc = jnp.dot(hi_ref[...], f[...], preferred_element_type=F32)
    acc += jnp.dot(lo_ref[...], f[...], preferred_element_type=F32)
    o_ref[...] = w_ref[...] - acc
    for b in range(width // block):
        kind = kind_ref[offset // block + b]

        @pl.when(kind < pivots)
        def _(b=b, kind=kind):
            for t in range(tile // block):
                flag = 1 - tiles_ref[(base + step) * (tile // block) + t, kind]
                at = (slice(t * block, (t + 1) * block), slice(b * block, (b + 1) * block))
                o_ref[at] = o_ref[at] * flag.astype(F32)


def main_step(where, kind, tiles, hi, lo, weights, pieces, out, offset, width, shard, block, pivots, part):
    rows, depth = hi.shape
    tile = min(TILE, rows)
    base = part * rows // tile
    chips = depth // shard // 2
    chunk = offset // width
    geo = (block, pivots, shard, chips, width, tile, offset, base)
    anywhere = pl.BlockSpec(memory_space=pl.ANY)
    in_specs = [
        pl.BlockSpec((tile, depth), lambda i, *_: (i, 0)),
        pl.BlockSpec((tile, depth), lambda i, *_: (i, 0)),
        pl.BlockSpec((tile, width), lambda i, *_: (base + i, chunk)),
    ] + [anywhere] * 4
    args = [where, kind, tiles, hi, lo, weights, *pieces]
    aliases = {}
    if out is not None:
        in_specs.append(anywhere)
        args.append(out)
        aliases = {len(args) - 1: 0}
    return pl.pallas_call(
        functools.partial(main_kernel, geo),
        grid_spec=pltpu.PrefetchScalarGridSpec(
            num_scalar_prefetch=3,
            grid=(rows // tile,),
            in_specs=in_specs,
            out_specs=pl.BlockSpec((tile, width), lambda i, *_: (base + i, chunk)),
            scratch_shapes=[
                pltpu.VMEM((depth, width), BF16),
                pltpu.SemaphoreType.DMA((2 * chips,)),
            ],
        ),
        out_shape=jax.ShapeDtypeStruct(weights.shape, F32),
        input_output_aliases=aliases,
        cost_estimate=pl.CostEstimate(
            flops=4 * rows * depth * width, bytes_accessed=8 * rows * width, transcendentals=0
        ),
        name="main",
    )(*args)


def program(n_col, n_row, weights, factor_rows, diag_inverse, prune_tiles, pivot_order):
    rows, cols = weights.shape
    pivots, block, _ = diag_inverse.shape
    shard = factor_rows.shape[0]
    blocks_dev = cols // block
    wide = n_col // 2
    chips = n_row // 2
    me_col = lax.axis_index("col")
    me_row = lax.axis_index("row")
    chip = me_row // 2

    def up(x, r):
        pairs = [(z * 2 + c, z * 2 + 2 + c) for z in range(r, chips - 1) for c in range(2)]
        return lax.ppermute(x, "row", pairs)

    def down(x, r):
        pairs = [(z * 2 + c, z * 2 - 2 + c) for z in range(1, chips - r) for c in range(2)]
        return lax.ppermute(x, "row", pairs)

    def sibling(x):
        return lax.ppermute(x, "row", [(i, i ^ 1) for i in range(n_row)])

    def gather(x, own_sibling):
        ups, downs = [x], [x]
        for r in range(chips - 1):
            ups.append(up(ups[-1], r))
            downs.append(down(downs[-1], r))
        parts = [
            jnp.where(chip >= q + 1, ups[q + 1], downs[chips - 1 - q]) for q in range(chips - 1)
        ]
        joined = jnp.concatenate(parts, axis=0)
        return own_sibling, joined, sibling(joined)

    def swap_lo(x):
        return lax.ppermute(x, "col", [(i, i ^ 1) for i in range(n_col)])

    def shift_hi(x, d):
        pairs = [(((h + d) % wide) * 2 + l, h * 2 + l) for h in range(wide) for l in range(2)]
        return lax.ppermute(x, "col", pairs)

    owner = pivot_order // blocks_dev
    local = pivot_order % blocks_dev
    ks = jnp.arange(pivots, dtype=jnp.int32)
    same = owner[:, None] == owner[None, :]
    rank = jnp.sum((same & (ks[None, :] < ks[:, None])).astype(jnp.int32), axis=1)
    mine = owner == me_col
    place = (rank[None, :] == ks[:, None]) & mine[None, :]
    index = jnp.sum(jnp.where(place, local[None, :], 0), axis=1)
    rel_hi = (owner // 2 - me_col // 2 + wide) % wide
    rel = rel_hi * 2 + (owner % 2 != me_col % 2).astype(jnp.int32)
    block_ids = jnp.arange(blocks_dev, dtype=jnp.int32)
    hit = (block_ids[:, None] == local[None, :]) & mine[None, :]
    kind = jnp.min(jnp.where(hit, ks[None, :], pivots), axis=1)
    where = jnp.stack([chip, me_row % 2]).astype(jnp.int32)

    f_pick = pick(factor_rows, local, mine.astype(jnp.int32), block)
    f_pick = f_pick + swap_lo(f_pick)
    f_here = f_pick
    for d in range(1, wide):
        f_here = f_here + shift_hi(f_pick, d)
    f_pieces = (f_here,) + gather(f_here, sibling(f_here))

    def exchange(index, count, part):
        a, b = pack(weights, index, count, block, part)
        far = range(1, wide)
        a_lo = swap_lo(a)
        b_hi = [shift_hi(b, d) for d in far]
        b_lo = swap_lo(b)
        a_hi = [shift_hi(a, d) for d in far]
        a_far = [shift_hi(a_lo, d) for d in far]
        b_far = [swap_lo(x) for x in b_hi]
        a_all = [a, a_lo]
        b_all = [b, b_lo]
        for d in range(wide - 1):
            a_all += [a_hi[d], a_far[d]]
            b_all += [b_hi[d], b_far[d]]
        return a_all + b_all

    count = (pivots + 1) // 2
    crowded = jnp.max(rank) >= count
    errors = []
    for part in range(2):
        near = exchange(index[:count], count, part)

        def run(sources, part=part):
            return chain(
                count, rel, rank, prune_tiles, where, sources, f_pieces, diag_inverse,
                rows // 2, shard, part,
            )

        def few(near=near, run=run):
            return run([near])

        def many(near=near, run=run, part=part):
            return run([near, exchange(index[count:], count, part)])

        errors.append(lax.cond(crowded, many, few))

    widths = [cols // 2, cols // 2]
    sown = sibling(factor_rows)
    out = None
    offset = 0
    for width in widths:
        far = gather(factor_rows[:, offset : offset + width], sown)
        for part in range(2):
            hi, lo = errors[part]
            out = main_step(
                where, kind, prune_tiles, hi, lo, weights, (factor_rows,) + far, out, offset,
                width, shard, block, pivots, part,
            )
        offset += width
    return out


def solution(mesh):
    n_col, n_row = mesh.shape["col"], mesh.shape["row"]
    return jax.shard_map(
        functools.partial(program, n_col, n_row),
        mesh=mesh,
        in_specs=(P("row", "col"), P("row", "col"), P(), P("row", None), P()),
        out_specs=P("row", "col"),
        check_vma=False,
    )
```

```python
import functools

import jax
import jax.numpy as jnp
from jax import lax
from jax.experimental import pallas as pl
from jax.experimental.pallas import tpu as pltpu
from jax.sharding import PartitionSpec as P


F32 = jnp.float32
BF16 = jnp.bfloat16
TOP = 32767.0
TAIL = 16
TILE = 512


def eye_of(n):
    return lax.broadcasted_iota(jnp.int32, (n, n), 0) == lax.broadcasted_iota(jnp.int32, (n, n), 1)


def pack_kernel(block, half, idx_ref, w_ref, a_ref, b_ref):
    for part, out in enumerate((a_ref, b_ref)):
        x = w_ref[part * half : (part + 1) * half, :]
        top = jnp.maximum(jnp.max(jnp.abs(x), axis=1, keepdims=True), 1e-30)
        level = jnp.ceil(jnp.log2(top))
        coded = jnp.clip(jnp.round(x * (TOP * jnp.exp2(-level))), -TOP, TOP)
        out[0, :half, :] = coded.astype(jnp.int32).astype(jnp.int16)
        tail = jnp.zeros((TAIL, block), F32)
        row = lax.broadcasted_iota(jnp.int32, (TAIL, block), 0)
        for t in range(half // block):
            spread = jnp.where(eye_of(block), level[t * block : (t + 1) * block], 0.0)
            line = jnp.sum(spread, axis=0, keepdims=True)
            tail = jnp.where(row == t, line, tail)
        out[0, half:, :] = tail.astype(jnp.int32).astype(jnp.int16)


def pack(weights, index, count, block, part):
    rows = weights.shape[0] // 2
    half = rows // 2
    shape = jax.ShapeDtypeStruct((count, half + TAIL, block), jnp.int16)
    return pl.pallas_call(
        functools.partial(pack_kernel, block, half),
        grid_spec=pltpu.PrefetchScalarGridSpec(
            num_scalar_prefetch=1,
            grid=(count,),
            in_specs=[pl.BlockSpec((rows, block), lambda m, idx: (part, idx[m]))],
            out_specs=[pl.BlockSpec((1, half + TAIL, block), lambda m, idx: (m, 0, 0))] * 2,
        ),
        out_shape=[shape, shape],
        name="pack",
    )(index, weights)


def gather_rows(chip, core, chips, shard, pieces, span, far_span, target, sems):
    own, sown, far, sfar = pieces
    todo = [(own.at[:, span], chip * 2 + core), (sown.at[:, span], chip * 2 + 1 - core)]
    for q in range(chips - 1):
        there = lax.rem(chip - q - 1 + chips, chips)
        todo.append((far.at[pl.ds(q * shard, shard), far_span], there * 2 + core))
        todo.append((sfar.at[pl.ds(q * shard, shard), far_span], there * 2 + 1 - core))
    return [
        pltpu.make_async_copy(
            src, target.at[pl.ds(pl.multiple_of(at * shard, shard), shard), :], sems.at[n]
        )
        for n, (src, at) in enumerate(todo)
    ]


def chain_kernel(geo, *refs):
    groups, n_rel, count, pivots, block, tile, half, shard, base = geo
    rel_ref, rank_ref, tiles_ref, where_ref = refs[:4]
    n_src = groups * 2 * n_rel
    sources = refs[4 : 4 + n_src]
    f_pieces = refs[4 + n_src : 8 + n_src]
    d_ref, hi_ref, lo_ref, coded, tails, cur, f_all, sems, f_sems = refs[8 + n_src :]
    sub = tile // block
    depth = pivots * block
    chips = depth // shard // 2

    def f_copies():
        span = pl.ds(0, depth)
        return gather_rows(
            where_ref[0], where_ref[1], chips, shard, f_pieces, span, span, f_all, f_sems
        )

    def copies(k, ref, part):
        rank = lax.rem(rank_ref[k], count)
        return (
            pltpu.make_async_copy(
                ref.at[rank, pl.ds(0, half), :],
                coded.at[k, pl.ds(part * half, half), :],
                sems.at[part, k],
            ),
            pltpu.make_async_copy(
                ref.at[rank, pl.ds(half, TAIL), :],
                tails.at[k, pl.ds(part * TAIL, TAIL), :],
                sems.at[2 + part, k],
            ),
        )

    @pl.loop(0, pivots)
    def _(k):
        for group in range(groups):
            for part in range(2):
                for rel in range(n_rel):
                    ref = sources[(group * 2 + part) * n_rel + rel]

                    @pl.when((rel_ref[k] == rel) & (rank_ref[k] // count == group))
                    def _(ref=ref, part=part):
                        for copy in copies(k, ref, part):
                            copy.start()

    for copy in f_copies():
        copy.start()

    eye = eye_of(block)
    for k in range(pivots):
        for part in range(2):
            for copy in copies(k, sources[0], part):
                copy.wait()
        tail = tails[k].astype(jnp.int32).astype(F32)
        for t in range(sub):
            here = t // (half // block) * TAIL + t % (half // block)
            line = tail[here : here + 1, :]
            level = jnp.sum(jnp.where(eye, line, 0.0), axis=1, keepdims=True)
            span = slice(t * block, (t + 1) * block)
            value = coded[k, span, :].astype(jnp.int32).astype(F32)
            cur[span, k * block : (k + 1) * block] = value * (jnp.exp2(level) * (1.0 / TOP))

    for copy in f_copies():
        copy.wait()
    for k in range(pivots):
        cols = slice(k * block, (k + 1) * block)
        now = cur[:, cols]
        now_hi = now.astype(BF16)
        now_lo = (now - now_hi.astype(F32)).astype(BF16)
        diag = d_ref[k]
        err = jnp.dot(
            jnp.concatenate([now_hi, now_lo], axis=1),
            jnp.concatenate([diag, diag], axis=0),
            preferred_element_type=F32,
        )
        parts = []
        for t in range(sub):
            flag = tiles_ref[base + t, k].astype(F32)
            parts.append(err[t * block : (t + 1) * block] * flag)
        err = jnp.concatenate(parts, axis=0)
        hi = err.astype(BF16)
        lo = (err - hi.astype(F32)).astype(BF16)
        hi_ref[:, cols] = hi
        lo_ref[:, cols] = lo
        if k + 1 < pivots:
            f = f_all[cols, (k + 1) * block :]
            both = jnp.concatenate([hi, lo], axis=1)
            cur[:, (k + 1) * block :] -= jnp.dot(
                both, jnp.concatenate([f, f], axis=0), preferred_element_type=F32
            )


def chain(count, rel, rank, tiles, where, sources, f_pieces, diag, rows, shard, part):
    pivots, block, _ = diag.shape
    half = rows // 2
    tile = rows
    groups = len(sources)
    n_rel = len(sources[0]) // 2
    flat = [x for group in sources for x in group]
    depth = pivots * block
    shape = jax.ShapeDtypeStruct((rows, depth), BF16)
    anywhere = pl.BlockSpec(memory_space=pl.ANY)
    geo = (groups, n_rel, count, pivots, block, tile, half, shard, part * rows // block)
    return pl.pallas_call(
        functools.partial(chain_kernel, geo),
        grid_spec=pltpu.PrefetchScalarGridSpec(
            num_scalar_prefetch=4,
            grid=(rows // tile,),
            in_specs=[anywhere] * (len(flat) + 4)
            + [pl.BlockSpec(diag.shape, lambda i, *_: (0, 0, 0))],
            out_specs=[pl.BlockSpec((tile, depth), lambda i, *_: (i, 0))] * 2,
            scratch_shapes=[
                pltpu.VMEM((pivots, tile, block), jnp.int16),
                pltpu.VMEM((pivots, 2 * TAIL, block), jnp.int16),
                pltpu.VMEM((tile, depth), F32),
                pltpu.VMEM((depth, depth), BF16),
                pltpu.SemaphoreType.DMA((4, pivots)),
                pltpu.SemaphoreType.DMA((depth // shard,)),
            ],
        ),
        out_shape=[shape, shape],
        cost_estimate=pl.CostEstimate(
            flops=4 * rows * depth * depth, bytes_accessed=8 * rows * depth, transcendentals=0
        ),
        name="chain",
    )(rel, rank, tiles, where, *flat, *f_pieces, diag)


def pick_kernel(pivots, block, local_ref, mine_ref, f_ref, o_ref):
    for k in range(pivots):
        cols = pl.ds(pl.multiple_of(local_ref[k] * block, block), block)
        part = f_ref[:, cols].astype(F32) * mine_ref[k].astype(F32)
        o_ref[:, k * block : (k + 1) * block] = part.astype(BF16)


def pick(factor_rows, local, mine, block):
    shard, cols = factor_rows.shape
    pivots = local.shape[0]
    return pl.pallas_call(
        functools.partial(pick_kernel, pivots, block),
        grid_spec=pltpu.PrefetchScalarGridSpec(
            num_scalar_prefetch=2,
            grid=(1,),
            in_specs=[pl.BlockSpec((shard, cols), lambda i, *_: (0, 0))],
            out_specs=pl.BlockSpec((shard, pivots * block), lambda i, *_: (0, 0)),
        ),
        out_shape=jax.ShapeDtypeStruct((shard, pivots * block), BF16),
        name="pick",
    )(local, mine, factor_rows)


def main_kernel(geo, where_ref, kind_ref, tiles_ref, hi_ref, lo_ref, w_ref, *refs):
    block, pivots, shard, chips, tile, offset, base = geo
    o_ref, f_all, sems = refs[-3:]
    step = pl.program_id(0)
    steps = pl.num_programs(0)
    slot = lax.rem(step, 2)
    f = f_all.at[slot]

    def copies(j):
        here = lax.rem(j, 2)
        at = pl.multiple_of(offset + j * tile, tile)
        far_at = pl.multiple_of(j * tile, tile)
        return gather_rows(
            where_ref[0], where_ref[1], chips, shard, refs[:4], pl.ds(at, tile),
            pl.ds(far_at, tile), f_all.at[here], sems.at[here],
        )

    @pl.when(step == 0)
    def _():
        for copy in copies(0):
            copy.start()

    @pl.when(step + 1 < steps)
    def _():
        for copy in copies(step + 1):
            copy.start()

    for copy in copies(step):
        copy.wait()
    first = offset // block + step * (tile // block)
    row = lax.broadcasted_iota(jnp.int32, (pivots * block, block), 0)
    for b in range(tile // block):
        kind = kind_ref[first + b]

        @pl.when(kind < pivots)
        def _(b=b, kind=kind):
            cols = slice(b * block, (b + 1) * block)
            f[:, cols] = jnp.where(row < kind * block, f[:, cols].astype(F32), 0.0).astype(BF16)

    acc = jnp.dot(hi_ref[...], f[...], preferred_element_type=F32)
    acc += jnp.dot(lo_ref[...], f[...], preferred_element_type=F32)
    o_ref[...] = w_ref[...] - acc
    for b in range(tile // block):
        kind = kind_ref[first + b]

        @pl.when(kind < pivots)
        def _(b=b, kind=kind):
            for t in range(o_ref.shape[0] // block):
                flag = 1 - tiles_ref[base + t, kind]
                at = (slice(t * block, (t + 1) * block), slice(b * block, (b + 1) * block))
                o_ref[at] = o_ref[at] * flag.astype(F32)


def main_step(
    where, kind, tiles, hi, lo, weights, pieces, out, offset, width, shard, block, pivots, part
):
    rows, depth = hi.shape
    tile = min(TILE, width)
    chips = depth // shard // 2
    lead = offset // tile
    geo = (block, pivots, shard, chips, tile, offset, part * rows // block)
    anywhere = pl.BlockSpec(memory_space=pl.ANY)
    in_specs = [
        pl.BlockSpec((rows, depth), lambda j, *_: (0, 0)),
        pl.BlockSpec((rows, depth), lambda j, *_: (0, 0)),
        pl.BlockSpec((rows, tile), lambda j, *_: (part, lead + j)),
    ] + [anywhere] * 4
    args = [where, kind, tiles, hi, lo, weights, *pieces]
    aliases = {}
    if out is not None:
        in_specs.append(anywhere)
        args.append(out)
        aliases = {len(args) - 1: 0}
    return pl.pallas_call(
        functools.partial(main_kernel, geo),
        grid_spec=pltpu.PrefetchScalarGridSpec(
            num_scalar_prefetch=3,
            grid=(width // tile,),
            in_specs=in_specs,
            out_specs=pl.BlockSpec((rows, tile), lambda j, *_: (part, lead + j)),
            scratch_shapes=[
                pltpu.VMEM((2, depth, tile), BF16),
                pltpu.SemaphoreType.DMA((2, 2 * chips)),
            ],
        ),
        out_shape=jax.ShapeDtypeStruct(weights.shape, F32),
        input_output_aliases=aliases,
        cost_estimate=pl.CostEstimate(
            flops=4 * rows * depth * width, bytes_accessed=8 * rows * width, transcendentals=0
        ),
        name="main",
    )(*args)


def program(n_col, n_row, weights, factor_rows, diag_inverse, prune_tiles, pivot_order):
    rows, cols = weights.shape
    pivots, block, _ = diag_inverse.shape
    shard = factor_rows.shape[0]
    blocks_dev = cols // block
    wide = n_col // 2
    chips = n_row // 2
    me_col = lax.axis_index("col")
    me_row = lax.axis_index("row")
    chip = me_row // 2

    def up(x, r):
        pairs = [(z * 2 + c, z * 2 + 2 + c) for z in range(r, chips - 1) for c in range(2)]
        return lax.ppermute(x, "row", pairs)

    def down(x, r):
        pairs = [(z * 2 + c, z * 2 - 2 + c) for z in range(1, chips - r) for c in range(2)]
        return lax.ppermute(x, "row", pairs)

    def sibling(x):
        return lax.ppermute(x, "row", [(i, i ^ 1) for i in range(n_row)])

    def gather(x, own_sibling):
        ups, downs = [x], [x]
        for r in range(chips - 1):
            ups.append(up(ups[-1], r))
            downs.append(down(downs[-1], r))
        parts = [
            jnp.where(chip >= q + 1, ups[q + 1], downs[chips - 1 - q])
            for q in range(chips - 1)
        ]
        joined = jnp.concatenate(parts, axis=0)
        return own_sibling, joined, sibling(joined)

    def swap_lo(x):
        return lax.ppermute(x, "col", [(i, i ^ 1) for i in range(n_col)])

    def shift_hi(x, d):
        pairs = [(((h + d) % wide) * 2 + l, h * 2 + l) for h in range(wide) for l in range(2)]
        return lax.ppermute(x, "col", pairs)

    owner = pivot_order // blocks_dev
    local = pivot_order % blocks_dev
    ks = jnp.arange(pivots, dtype=jnp.int32)
    same = owner[:, None] == owner[None, :]
    rank = jnp.sum((same & (ks[None, :] < ks[:, None])).astype(jnp.int32), axis=1)
    mine = owner == me_col
    place = (rank[None, :] == ks[:, None]) & mine[None, :]
    index = jnp.sum(jnp.where(place, local[None, :], 0), axis=1)
    rel_hi = (owner // 2 - me_col // 2 + wide) % wide
    rel = rel_hi * 2 + (owner % 2 != me_col % 2).astype(jnp.int32)
    block_ids = jnp.arange(blocks_dev, dtype=jnp.int32)
    hit = (block_ids[:, None] == local[None, :]) & mine[None, :]
    kind = jnp.min(jnp.where(hit, ks[None, :], pivots), axis=1)
    where = jnp.stack([chip, me_row % 2]).astype(jnp.int32)

    f_pick = pick(factor_rows, local, mine.astype(jnp.int32), block)
    f_pick = f_pick + swap_lo(f_pick)
    f_here = f_pick
    for d in range(1, wide):
        f_here = f_here + shift_hi(f_pick, d)
    f_pieces = (f_here,) + gather(f_here, sibling(f_here))

    def exchange(index, count, part):
        a, b = pack(weights, index, count, block, part)
        far = range(1, wide)
        a_lo = swap_lo(a)
        b_hi = [shift_hi(b, d) for d in far]
        b_lo = swap_lo(b)
        a_hi = [shift_hi(a, d) for d in far]
        a_far = [shift_hi(a_lo, d) for d in far]
        b_far = [swap_lo(x) for x in b_hi]
        a_all = [a, a_lo]
        b_all = [b, b_lo]
        for d in range(wide - 1):
            a_all += [a_hi[d], a_far[d]]
            b_all += [b_hi[d], b_far[d]]
        return a_all + b_all

    count = (pivots + 1) // 2
    crowded = jnp.max(rank) >= count
    errors = []
    for part in range(2):
        near = exchange(index[:count], count, part)

        def run(sources, part=part):
            return chain(
                count, rel, rank, prune_tiles, where, sources, f_pieces, diag_inverse,
                rows // 2, shard, part,
            )

        def few(near=near, run=run):
            return run([near])

        def many(near=near, run=run, part=part):
            return run([near, exchange(index[count:], count, part)])

        errors.append(lax.cond(crowded, many, few))

    widths = [cols // 2, cols // 2]
    sown = sibling(factor_rows)
    out = None
    offset = 0
    for width in widths:
        far = gather(factor_rows[:, offset : offset + width], sown)
        for part in range(2):
            hi, lo = errors[part]
            out = main_step(
                where, kind, prune_tiles, hi, lo, weights, (factor_rows,) + far, out, offset,
                width, shard, block, pivots, part,
            )
        offset += width
    return out


def solution(mesh):
    n_col, n_row = mesh.shape["col"], mesh.shape["row"]
    return jax.shard_map(
        functools.partial(program, n_col, n_row),
        mesh=mesh,
        in_specs=(P("row", "col"), P("row", "col"), P(), P("row", None), P()),
        out_specs=P("row", "col"),
        check_vma=False,
    )
```
